32 devices in a mesh: col: 4 (over z), row: 8 (over y, x, core).
Axes of the slice: x: 2, y: 2, z: 4, core: 2. Of those that a mesh axis runs over, the one named last changes fastest.
Arguments:
- matrix: float32 [8192, 8192], P('row', 'col'), may hold values from -6 to 6
- pattern: int32 [32, 4], P('row'), may hold values 0 or 1
- active: int32 [8, 4, 24, 2], P('row', 'col'), may hold values from 0 to 7, as said below
- pivots: int32 [4], replicated, may hold values from 0 to 31, as said below
- lower_inv: float32 [4, 256, 256], replicated, may hold values from -0.3 to 0.3, as said below
- upper_inv: float32 [4, 256, 256], replicated, may hold values from -0.3 to 0.3, as said below
Outputs:
- factored: float32 [8192, 8192], P('row', 'col')
The draws below stay inside these ranges and needn't reach their ends.
Inputs may be any that keep to these rules, and one draw needn't show every extreme that they name: For each device (a, b), active[a, b] holds 24 distinct pairs (l, c) with l below 4 and c below 8. `pivots`: 4 distinct block rows of the window, among them always the first and the last block row. `lower_inv`: each block is lower triangular with a positive diagonal. `upper_inv`: each block is upper triangular with a positive diagonal.
All inputs are finite; a program needn't handle non-finite values. No bound on the sum of `pattern` on one device may be relied on, other than what follows from the above.
Results may differ from the reference program's by a relative error of at most 0.0001.
Values sent between devices are 32-bit elements; how exact they have to be, the bound alone decides.
A program may use at most 128 MiB of HBM per device.

```python
import jax
import jax.numpy as jnp
from jax import lax

BLOCK_SIZE = 256
PANELS = 4
RL = 4
CL = 8
ACT = 24
PR = 8
PC = 4
NR = 32
NC = 32


def draw_active(key, part):
    device_keys = jax.random.split(jax.random.fold_in(key, 3), PR * PC)

    def one_device(sub_key):
        chosen = jax.random.permutation(sub_key, RL * CL)[:ACT]
        return jnp.stack([chosen // CL, chosen % CL], axis=1).astype(jnp.int32)
    return jax.vmap(one_device)(device_keys).reshape(PR, PC, ACT, 2)


def draw_pivots(key, part):
    middle = jax.random.permutation(jax.random.fold_in(key, 5), NR - 2)[:PANELS - 2].astype(jnp.int32) + 1
    ends = jnp.array([0, NR - 1], dtype=jnp.int32)
    chosen = jnp.concatenate([ends, middle])
    order = jax.random.permutation(jax.random.fold_in(key, 6), PANELS)
    return chosen[order].astype(jnp.int32)


def inverse_blocks(key, lower_side):
    noise_key = jax.random.fold_in(key, 11)
    gain_key = jax.random.fold_in(key, 12)
    noise = jax.random.normal(noise_key, (PANELS, BLOCK_SIZE, BLOCK_SIZE), jnp.float32)
    noise = jnp.clip(noise, -4.0, 4.0) * (0.6 / BLOCK_SIZE ** 0.5)
    if lower_side:
        noise = jnp.tril(noise, -1)
    else:
        noise = jnp.triu(noise, 1)
    gains = jax.random.uniform(gain_key, (PANELS, 1, BLOCK_SIZE), jnp.float32, 0.6, 1.4)
    return 0.2 * (jnp.eye(BLOCK_SIZE, dtype=jnp.float32)[None] * gains + noise)


def draw_lower_inv(key, part):
    return inverse_blocks(jax.random.fold_in(key, 21), True)


def draw_upper_inv(key, part):
    return inverse_blocks(jax.random.fold_in(key, 22), False)


def touch_ends(drawn, key, smallest, largest):
    longest = drawn.shape.index(max(drawn.shape))
    spots = []
    for shift in (0, 1):
        where = [jax.random.randint(jax.random.fold_in(key, axis), (), 0, length) for axis, length in enumerate(drawn.shape)]
        where[longest] = (where[longest] + shift) % drawn.shape[longest]
        spots.append(tuple(where))
    return drawn.at[spots[0]].set(smallest).at[spots[1]].set(largest)


def level_of(rng, dims, pieces, low, largest):
    factor_of = 1.0
    for position, parts in pieces:
        draws = jax.random.uniform(jax.random.fold_in(jax.random.fold_in(rng, 6), position), (parts,), jnp.float32, low / len(pieces), largest / len(pieces))
        factor_of = factor_of * jnp.repeat(jnp.exp(draws), dims[position] // parts).reshape((-1,) + (1,) * (len(dims) - 1 - position))
    return factor_of


def centred(rng, extent, scale, bound, cuts=(), held_as=jnp.bfloat16):
    entries = jax.random.normal(rng, extent, jnp.float32) * scale
    if len(cuts) > 0:
        entries = level_of(rng, extent, cuts, -0.22, 0.18) * entries
    return jnp.clip(entries, min=-bound, max=bound).astype(held_as)


def setup_inputs(seed: int = 0) -> dict:
    arg_keys = jax.random.split(jax.random.key(seed), 7)
    return {
        "matrix": centred(arg_keys[0], (NR * BLOCK_SIZE, NC * BLOCK_SIZE), 1.0, 6.0, ((0, 8), (1, 4)), jnp.float32),
        "pattern": touch_ends((jax.random.randint(arg_keys[1], (NR, PANELS), 0, 4) < 3).astype(jnp.int32), jax.random.fold_in(arg_keys[1], 1), 0, 1),
        "active": draw_active(jax.random.fold_in(arg_keys[6], 71), 0),
        "pivots": draw_pivots(jax.random.fold_in(arg_keys[6], 71), 0),
        "lower_inv": draw_lower_inv(jax.random.fold_in(arg_keys[6], 71), 0),
        "upper_inv": draw_upper_inv(jax.random.fold_in(arg_keys[6], 71), 0),
    }


def reference(matrix, pattern, active, pivots, lower_inv, upper_inv):
    highest = lax.Precision.HIGHEST
    dev_rows = jnp.arange(PR, dtype=jnp.int32)[:, None, None]
    dev_cols = jnp.arange(PC, dtype=jnp.int32)[None, :, None]
    live_rows = (dev_rows * RL + active[:, :, :, 0]).reshape(-1).astype(jnp.int32)
    live_cols = (dev_cols * CL + active[:, :, :, 1]).reshape(-1).astype(jnp.int32)
    remaining_tiles = jnp.zeros((NR, NC), jnp.int32).at[live_rows, live_cols].set(1)
    block_row_count = jnp.arange(NR, dtype=jnp.int32)
    block_cols = jnp.arange(NC, dtype=jnp.int32)
    factored = matrix
    for present_panel in range(PANELS):
        elimination_rows = jnp.any(block_row_count[:, None] == pivots[None, :present_panel + 1], axis=1)
        finished_columns = (block_cols % CL == 0) & (block_cols // CL <= present_panel)
        column = present_panel * CL
        raw_col = factored[:, column * BLOCK_SIZE:(column + 1) * BLOCK_SIZE]
        keep_mask = jnp.repeat((pattern[:, present_panel] != 0).astype(jnp.float32), BLOCK_SIZE)[:, None]
        lower_tile_grid = jnp.dot(raw_col, upper_inv[present_panel], precision=highest, preferred_element_type=jnp.float32) * keep_mask
        pivot_row = pivots[present_panel].astype(jnp.int32)
        raw_row = lax.dynamic_slice_in_dim(factored, pivot_row * BLOCK_SIZE, BLOCK_SIZE, 0)
        upper_tiles = jnp.dot(lower_inv[present_panel], raw_row, precision=highest, preferred_element_type=jnp.float32)
        permitted_entries = (remaining_tiles != 0) & jnp.logical_not(elimination_rows)[:, None] & jnp.logical_not(finished_columns)[None, :]

        def update_row(row_item):
            row_block, low_tile, row_ok = row_item
            product = jnp.dot(low_tile, upper_tiles, precision=highest, preferred_element_type=jnp.float32)
            return row_block - jnp.where(jnp.repeat(row_ok, BLOCK_SIZE)[None, :], product, 0.0)

        updated = lax.map(update_row, (factored.reshape(NR, BLOCK_SIZE, NC * BLOCK_SIZE), lower_tile_grid.reshape(NR, BLOCK_SIZE, BLOCK_SIZE), permitted_entries))
        factored = updated.reshape(NR * BLOCK_SIZE, NC * BLOCK_SIZE)
        column_present = factored[:, column * BLOCK_SIZE:(column + 1) * BLOCK_SIZE]
        fresh_column = jnp.where(jnp.repeat(jnp.logical_not(elimination_rows), BLOCK_SIZE)[:, None], lower_tile_grid, column_present)
        factored = factored.at[:, column * BLOCK_SIZE:(column + 1) * BLOCK_SIZE].set(fresh_column)
        row_now = lax.dynamic_slice_in_dim(factored, pivot_row * BLOCK_SIZE, BLOCK_SIZE, 0)
        new_row = jnp.where(jnp.repeat(jnp.logical_not(finished_columns), BLOCK_SIZE)[None, :], upper_tiles, row_now)
        factored = lax.dynamic_update_slice_in_dim(factored, new_row, pivot_row * BLOCK_SIZE, 0)
    return factored
```

```python
import functools

import jax
import jax.numpy as jnp
from jax import lax
from jax.experimental import pallas as pl
from jax.experimental.pallas import tpu as pltpu
from jax.sharding import PartitionSpec as P


def when(cond, fn):
    pl.when(cond)(fn)


def loop(low, high, fn):
    def one(index, carry):
        fn(index)
        return carry

    lax.fori_loop(low, high, one, 0)


def ranked(piv):
    a, b = jnp.minimum(piv[0], piv[1]), jnp.maximum(piv[0], piv[1])
    c, d = jnp.minimum(piv[2], piv[3]), jnp.maximum(piv[2], piv[3])
    e, f = jnp.maximum(a, c), jnp.minimum(b, d)
    return jnp.minimum(e, f), jnp.maximum(e, f)


def comm_kernel(
    dims, axes, hits, meta, mat, rows, strips, cross, metas,
    matv, send1, recv1, buf2, recv2, homev,
    m_send, m_recv, z_send, z_recv, ab_send, ab_recv, one_send, one_recv,
    two_send, two_recv, ag_send, ag_recv, xs_send, xs_recv, xz_send, xz_recv, local,
):
    panels, tile, r_loc, width, rsize, csize = dims
    chips = rsize // 2
    w = width // rsize
    rr = tile // rsize
    holders = tile // w
    last = panels - 1
    me = lax.axis_index("row")
    plane = lax.axis_index("col")
    chip, core = me // 2, me % 2
    lin = plane * rsize + me
    square = chips == 4

    def dev(row, col):
        return tuple(row if name == "row" else col for name in axes)

    def remote(src, dst, ssem, rsem, row, col):
        return pltpu.make_async_remote_copy(
            src_ref=src, dst_ref=dst, send_sem=ssem, recv_sem=rsem,
            device_id=dev(row, col), device_id_type=pl.DeviceIdType.MESH,
        )

    if square:
        x, y = chip % 2, chip // 2
        xn, yn = chip + 1 - 2 * x, chip + 2 - 4 * y
        to_chip = from_chip = [xn, yn, 3 - chip]
    else:
        to_chip = [(chip + d) % chips for d in range(1, chips)]
        from_chip = [(chip - d + chips) % chips for d in range(1, chips)]
    sib = chip * 2 + 1 - core

    def meta_copy(t):
        return remote(meta, metas.at[lin], m_send.at[t], m_recv.at[lin], t % rsize, t // rsize)

    def meta_in(t):
        return remote(meta, metas.at[t], m_send.at[t], m_recv.at[t], t % rsize, t // rsize)

    loop(0, rsize * csize, lambda t: when(t != lin, lambda: meta_copy(t).start()))
    own_meta = pltpu.make_async_copy(meta, metas.at[lin], local.at[0])
    own_meta.start()

    def z_rows(r):
        return pl.ds(pl.multiple_of(r * tile, tile), tile)

    def z_own(r, up):
        return remote(
            mat.at[z_rows(r), pl.ds(0, tile)], strips.at[plane, z_rows(r)],
            z_send.at[1 - up, plane, r], z_recv.at[1 - up, plane, r], me, plane + 2 * up - 1,
        )

    def z_pass(n, r, up):
        return remote(
            strips.at[n, z_rows(r)], strips.at[n, z_rows(r)],
            z_send.at[1 - up, n, r], z_recv.at[1 - up, n, r], me, plane + 2 * up - 1,
        )

    is_holder = plane < panels

    def z_start(r):
        when(is_holder & (plane + 1 < csize), lambda: z_own(r, 1).start())
        when(is_holder & (plane > 0), lambda: z_own(r, 0).start())

    loop(0, r_loc, z_start)

    def z_relay(p, r):
        low, high = plane - p, plane + p

        def from_low():
            z_pass(low, r, 1).wait_recv()
            when(plane + 1 < csize, lambda: z_pass(low, r, 1).start())

        def from_high():
            z_pass(high, r, 0).wait_recv()
            when(plane > 0, lambda: z_pass(high, r, 0).start())

        when((low >= 0) & (low < panels), from_low)
        when(high < panels, from_high)

    def z_drain(p, r):
        low, high = plane - p, plane + p
        if p == 0:
            when(is_holder & (plane + 1 < csize), lambda: z_own(r, 1).wait_send())
            when(is_holder & (plane > 0), lambda: z_own(r, 0).wait_send())
        else:
            when((low >= 0) & (low < panels) & (plane + 1 < csize), lambda: z_pass(low, r, 1).wait_send())
            when((high < panels) & (plane > 0), lambda: z_pass(high, r, 0).wait_send())

    load = pltpu.make_async_copy(mat, matv, local.at[1])
    load.start()

    def cols_at(a):
        return pl.ds(pl.multiple_of(a * w, w), w)

    def fixed(slot, root):
        base = 0 if slot == 0 else (r_loc - 1) * tile

        def to(a):
            return remote(
                mat.at[pl.ds(base, tile), cols_at(a)], rows.at[a, slot],
                ab_send.at[slot, a], ab_recv.at[slot], a, plane,
            )

        return to

    top, bottom = fixed(0, 0), fixed(last, rsize - 1)
    when(me == 0, lambda: loop(1, rsize, lambda a: top(a).start()))
    when(me == rsize - 1, lambda: loop(0, rsize - 1, lambda a: bottom(a).start()))

    load.wait()
    high_core = (core == 0).astype(jnp.float32)
    low_core = 1.0 - high_core
    step = 32

    def one(s):
        return remote(send1.at[s], recv1.at[s], one_send.at[s], one_recv.at[s], sib, plane)

    def pick(part):
        at = pl.ds(pl.multiple_of(part * step, step), step)
        for q in range(chips):
            even, odd = [], []
            for r in range(r_loc):
                there = pl.ds(pl.multiple_of(r * tile + part * step, step), step)
                even.append(matv[there, 2 * q * w : (2 * q + 1) * w])
                odd.append(matv[there, (2 * q + 1) * w : (2 * q + 2) * w])
            for s in range(2):
                left = sum(even[r] * hits[s, r] for r in range(r_loc))
                right = sum(odd[r] * hits[s, r] for r in range(r_loc))
                send1[s, q, at] = left * low_core + right * high_core
                buf2[s, q, at] = left * high_core + right * low_core

    loop(0, tile // step, pick)
    for s in range(2):
        one(s).start()
    own_slot = pltpu.make_async_copy(matv.at[pl.ds(0, tile), pl.ds(0, w)], rows.at[0, 0], local.at[2])
    own_last = pltpu.make_async_copy(
        matv.at[pl.ds((r_loc - 1) * tile, tile), pl.ds((rsize - 1) * w, w)], rows.at[rsize - 1, last], local.at[2]
    )
    own_strip = pltpu.make_async_copy(matv.at[:, pl.ds(0, tile)], strips.at[plane], local.at[3])
    when(me == 0, lambda: own_slot.start())
    when(me == rsize - 1, lambda: own_last.start())
    when(is_holder, lambda: own_strip.start())

    def two(s, d):
        return remote(
            buf2.at[s, to_chip[d]], recv2.at[s, d], two_send.at[s, d], two_recv.at[s, d],
            to_chip[d] * 2 + core, plane,
        )

    for s in range(2):
        one(s).wait_recv()
        for q in range(chips):
            buf2[s, q] = buf2[s, q] + recv1[s, q]
        for d in range(chips - 1):
            two(s, d).start()
    for r in range(2):
        z_relay(1, r)

    def region(a, c):
        return rows.at[a, c]

    def x_region(a, n):
        return cross.at[n, :, pl.ds(pl.multiple_of(a * rr, rr), rr), :]

    def ag(part, c, kind, a, row):
        ref = region(a, c) if part == 0 else x_region(a, c)
        return remote(ref, ref, ag_send.at[part, kind, c], ag_recv.at[part, kind, c], row, plane)

    direct = 2 if square else chips - 1
    sib_own = chips - 1

    def ag_start(part, c):
        ag(part, c, sib_own, me, sib).start()
        for d in range(direct):
            ag(part, c, d, me, to_chip[d] * 2 + core).start()

    def ag_own_wait(part, c):
        ag(part, c, sib_own, me, sib).wait_send()
        for d in range(direct):
            ag(part, c, d, me, to_chip[d] * 2 + core).wait_send()

    def peer(d):
        return from_chip[d] * 2 + core

    def ag_forward(part, c, first):
        for d in range(direct):
            ag(part, c, d, peer(d), sib).wait_recv()
            if square and first == (d == 0):
                ag(part, c, 2, peer(d), to_chip[1 - d] * 2 + core).start()
            ag(part, c, chips + d, peer(d), sib).start()

    def ag_far(part, c):
        if square:
            ag(part, c, 2, peer(2), sib).wait_recv()
            ag(part, c, chips + 2, peer(2), sib).start()

    def ag_end(part, c, first):
        for d in range(chips):
            kind = sib_own if d == chips - 1 else chips + d
            ag(part, c, kind, sib if d == chips - 1 else from_chip[d] * 2 + 1 - core, sib).wait_recv()
        ag_own_wait(part, c)
        for d in range(chips - 1):
            ag(part, c, chips + d, peer(d), sib).wait_send()
        if square:
            d = 0 if first else 1
            ag(part, c, 2, peer(d), to_chip[1 - d] * 2 + core).wait_send()

    def fixed_in(slot, root, own):
        when(me != root, lambda: (top if slot == 0 else bottom)(me).wait_recv())
        when(me == root, lambda: own.wait())

    for s in range(2):
        acc = buf2[s, chip]
        for d in range(chips - 1):
            two(s, d).wait_recv()
            acc = acc + recv2[s, d]
        homev[s] = acc
        put = pltpu.make_async_copy(homev.at[s], rows.at[me, s + 1], local.at[4 + s])
        put.start()
        put.wait()
        ag_start(0, s + 1)
        if s == 0:
            fixed_in(0, 0, own_slot)
            ag_start(0, 0)
            z_relay(1, 2)
        else:
            fixed_in(last, rsize - 1, own_last)
            ag_start(0, last)
            loop(3, r_loc, lambda r: z_relay(1, r))

    def xs(h, a):
        return remote(
            rows.at[h, :, pl.ds(pl.multiple_of(a * rr, rr), rr), :],
            cross.at[plane, :, pl.ds(pl.multiple_of(a * rr, rr), rr), pl.ds(h * w, w)],
            xs_send.at[h, a], xs_recv.at[h], a, plane,
        )

    for h in range(holders):
        own_x = pltpu.make_async_copy(
            rows.at[h, :, pl.ds(h * rr, rr), :],
            cross.at[plane, :, pl.ds(h * rr, rr), pl.ds(h * w, w)], local.at[6 + h],
        )

        def give(h=h, own_x=own_x):
            own_x.start()
            loop(0, rsize, lambda a: when(a != h, lambda: xs(h, a).start()))

        def take(h=h, own_x=own_x):
            when(me == h, lambda: own_x.wait())
            when(me != h, lambda: xs(h, me).wait_recv())

        when(is_holder & (me == h), give)
        when(is_holder, take)

    def xz(d):
        return remote(
            x_region(me, plane), x_region(me, plane), xz_send.at[d], xz_recv.at[plane],
            me, (plane + d) % csize,
        )

    when(is_holder, lambda: loop(1, csize, lambda d: xz(d).start()))

    half = panels // 2
    loop(0, half, lambda c: ag_forward(0, c, True))
    loop(half, panels, lambda c: ag_forward(0, c, False))
    for p in range(2, csize):
        loop(0, r_loc, lambda r, p=p: z_relay(p, r))

    def x_start(n):
        got = remote(x_region(me, n), x_region(me, n), xz_send.at[0], xz_recv.at[n], me, plane)
        when(plane != n, lambda: got.wait_recv())
        ag_start(1, n)

    loop(0, panels, x_start)
    loop(0, panels, lambda c: ag_far(0, c))
    loop(0, half, lambda c: ag_forward(1, c, True))
    loop(half, panels, lambda c: ag_forward(1, c, False))
    loop(0, panels, lambda c: ag_far(1, c))
    for part in range(2):
        loop(0, half, lambda c: ag_end(part, c, True))
        loop(half, panels, lambda c: ag_end(part, c, False))
    for p in range(csize):
        loop(0, r_loc, lambda r, p=p: z_drain(p, r))
    when(is_holder, lambda: loop(1, csize, lambda d: xz(d).wait_send()))
    for h in range(holders):
        when(
            is_holder & (me == h),
            lambda h=h: loop(0, rsize, lambda a: when(a != h, lambda: xs(h, a).wait_send())),
        )
    for s in range(2):
        one(s).wait_send()
        for d in range(chips - 1):
            two(s, d).wait_send()
    when(me == 0, lambda: loop(1, rsize, lambda a: top(a).wait_send()))
    when(me == rsize - 1, lambda: loop(0, rsize - 1, lambda a: bottom(a).wait_send()))
    when(is_holder, lambda: own_strip.wait())
    own_meta.wait()

    def meta_end(t):
        meta_copy(t).wait_send()
        meta_in(t).wait_recv()

    loop(0, rsize * csize, lambda t: when(t != lin, lambda: meta_end(t)))


def halves(value):
    high = value.astype(jnp.bfloat16)
    return high, (value - high.astype(jnp.float32)).astype(jnp.bfloat16)


def dot(left, right):
    return jnp.dot(left, right, preferred_element_type=jnp.float32)


def mm(left, right):
    (ah, al), (bh, bl) = left, right
    return dot(ah, bh) + dot(ah, bl) + dot(al, bh)


def lu_kernel(
    dims, piv, metas, mat, rows, strips, cross, linv, uinv, out,
    matv, rowv, stripv, crossv, lv, uv, linvs, uinvs, lows, ups, us, ls, lf, slot, sems, mat_sem,
):
    panels, tile, r_loc, width, rsize, csize = dims
    c_loc = width // tile
    w = width // rsize
    cells = r_loc * c_loc
    me = lax.axis_index("row")
    plane = lax.axis_index("col")

    def tile_at(ref, i, j):
        return ref.at[pl.ds(pl.multiple_of(i * tile, tile), tile), pl.ds(pl.multiple_of(j * tile, tile), tile)]

    loads = [
        pltpu.make_async_copy(cross, crossv, sems.at[0]),
        pltpu.make_async_copy(linv, lv, sems.at[1]),
        pltpu.make_async_copy(uinv, uv, sems.at[2]),
        pltpu.make_async_copy(strips, stripv, sems.at[3]),
    ]
    for load in loads:
        load.start()
    row_loads = []
    for a in range(rsize):
        j, off = divmod(a * w, tile)
        row_loads.append(pltpu.make_async_copy(rows.at[a], rowv.at[j, :, :, pl.ds(off, w)], sems.at[4 + a]))
        row_loads[-1].start()

    def mat_in(i, j):
        return pltpu.make_async_copy(tile_at(mat, i, j), matv.at[i, j], mat_sem.at[i, j])

    loop(0, r_loc, lambda i: loop(0, c_loc, lambda j: mat_in(i, j).start()))

    for k in range(panels):
        rank = jnp.int32(0)
        for m in range(panels):
            rank += (piv[m] < piv[k]).astype(jnp.int32)
        slot[k] = rank

    def live(row, col):
        device = (col // c_loc) * rsize + row // r_loc
        return metas[device, (row % r_loc) * c_loc + col % c_loc]

    def kept(row, k):
        device = row // r_loc
        return metas[device, cells + (row % r_loc) * panels + k]

    for load in loads[:3]:
        load.wait()

    def split_inv(k):
        linvs[0, k], linvs[1, k] = halves(lv[k])
        uinvs[0, k], uinvs[1, k] = halves(uv[k])

    loop(0, panels, split_inv)

    def pair(ref, *index):
        return ref[(0,) + index], ref[(1,) + index]

    def cross_panel(k):
        def low(m):
            value = mm(halves(crossv[k, slot[m]]), pair(uinvs, k)) * kept(piv[m], k)
            lows[0, m, k], lows[1, m, k] = halves(value)

        def up(n):
            value = mm(pair(linvs, k), halves(crossv[n, slot[k]]))
            ups[0, k, n], ups[1, k, n] = halves(value)

        loop(k + 1, panels, low)
        loop(k + 1, panels, up)

        def update(m):
            def one(n):
                def go():
                    crossv[n, slot[m]] = crossv[n, slot[m]] - mm(pair(lows, m, k), pair(ups, k, n))

                when((m != n) & (live(piv[m], n * c_loc) != 0), go)

            loop(k + 1, panels, one)

        loop(k + 1, panels, update)

    loop(0, panels - 1, cross_panel)
    for load in row_loads:
        load.wait()

    def row_column(j):
        def panel(k):
            value = mm(pair(linvs, k), halves(rowv[j, slot[k]]))
            rowv[j, slot[k]] = value
            closed = (j == 0) & (plane <= k)
            shown = value * jnp.where(closed, 0.0, 1.0).astype(jnp.float32)
            at = pl.ds(pl.multiple_of(k * tile, tile), tile)
            us[0, j, at], us[1, j, at] = halves(shown)

            def update(m):
                def go():
                    seen = (us[0, j, at], us[1, j, at])
                    rowv[j, slot[m]] = rowv[j, slot[m]] - mm(pair(lows, m, k), seen)

                when(jnp.logical_not(closed) & (live(piv[m], plane * c_loc + j) != 0), go)

            loop(k + 1, panels, update)

        loop(0, panels, panel)

    loop(0, c_loc, row_column)
    loads[3].wait()

    def row_tile(i):
        at = pl.ds(pl.multiple_of(i * tile, tile), tile)
        row = me * r_loc + i
        for k in range(panels):
            gone = row == piv[0]
            for m in range(1, k + 1):
                gone = gone | (row == piv[m])
            keep = jnp.where(gone, 0.0, 1.0).astype(jnp.float32)
            value = mm(halves(stripv[k, at]), pair(uinvs, k)) * kept(row, k)
            lf[k] = value
            ls[0, :, k * tile : (k + 1) * tile], ls[1, :, k * tile : (k + 1) * tile] = halves(value * keep)

            def update(n, k=k):
                def go():
                    left = (ls[0, :, k * tile : (k + 1) * tile], ls[1, :, k * tile : (k + 1) * tile])
                    stripv[n, at] = stripv[n, at] - mm(left, pair(ups, k, n))

                when(live(row, n * c_loc) != 0, go)

            loop(k + 1, panels, update)

        loop(0, c_loc, lambda j: mat_in(i, j).wait())

        def target(j):
            def go():
                matv[i, j] = matv[i, j] - mm((ls[0], ls[1]), pair(us, j))

            when(live(row, plane * c_loc + j) != 0, go)

        loop(0, c_loc, target)
        for k in range(panels):
            gone = row == piv[0]
            for m in range(1, k + 1):
                gone = gone | (row == piv[m])

            def put_low(k=k):
                matv[i, 0] = lf[k]

            when((plane == k) & jnp.logical_not(gone), put_low)

            def put_up(k=k):
                def one(j):
                    def go():
                        matv[i, j] = rowv[j, slot[k]]

                    when((j != 0) | (plane > k), go)

                loop(0, c_loc, one)

            when(row == piv[k], put_up)

        loop(0, c_loc, lambda j: mat_out(i, j).start())

    def mat_out(i, j):
        return pltpu.make_async_copy(matv.at[i, j], tile_at(out, i, j), mat_sem.at[i, j])

    loop(0, r_loc, row_tile)
    loop(0, r_loc, lambda i: loop(0, c_loc, lambda j: mat_out(i, j).wait()))


def body(mesh, matrix, pattern, active, pivots, lower_inv, upper_inv):
    panels, tile = lower_inv.shape[:2]
    height, width = matrix.shape
    r_loc, c_loc = height // tile, width // tile
    rsize, csize = mesh.shape["row"], mesh.shape["col"]
    chips, w = rsize // 2, width // rsize
    dims = (panels, tile, r_loc, width, rsize, csize)
    devices = rsize * csize
    cells = r_loc * c_loc
    spot = active[0, 0, :, 0] * c_loc + active[0, 0, :, 1]
    live = jnp.any(spot[:, None] == jnp.arange(cells, dtype=jnp.int32)[None, :], axis=0)
    meta = jnp.concatenate([live.astype(jnp.float32), (pattern != 0).astype(jnp.float32).reshape(-1)])
    meta = jnp.broadcast_to(jnp.pad(meta, (0, 128 - meta.shape[0]))[None, :], (8, 128))
    f32, bf16 = jnp.float32, jnp.bfloat16
    picked = jnp.stack(ranked(pivots))
    mine = lax.axis_index("row") * r_loc + jnp.arange(r_loc, dtype=jnp.int32)
    hits = (picked[:, None] == mine[None, :]).astype(f32)
    any_spec = pl.BlockSpec(memory_space=pl.ANY)
    smem = pl.BlockSpec(memory_space=pltpu.SMEM)
    dma = pltpu.SemaphoreType.DMA
    rows, strips, cross, metas = pl.pallas_call(
        functools.partial(comm_kernel, dims, tuple(mesh.axis_names)),
        out_shape=[
            jax.ShapeDtypeStruct((rsize, panels, tile, w), f32),
            jax.ShapeDtypeStruct((panels, height, tile), f32),
            jax.ShapeDtypeStruct((panels, panels, tile, tile), f32),
            jax.ShapeDtypeStruct((devices, 8, 128), f32),
        ],
        in_specs=[smem, any_spec, any_spec],
        out_specs=[any_spec] * 4,
        scratch_shapes=[
            pltpu.VMEM((height, width), f32),
            pltpu.VMEM((2, chips, tile, w), f32),
            pltpu.VMEM((2, chips, tile, w), f32),
            pltpu.VMEM((2, chips, tile, w), f32),
            pltpu.VMEM((2, chips - 1, tile, w), f32),
            pltpu.VMEM((2, tile, w), f32),
            dma((devices,)), dma((devices,)),
            dma((2, panels, r_loc)), dma((2, panels, r_loc)),
            dma((panels, rsize)), dma((panels,)),
            dma((2,)), dma((2,)),
            dma((2, chips)), dma((2, chips)),
            dma((2, 2 * chips, panels)), dma((2, 2 * chips, panels)),
            dma((tile // w, rsize)), dma((tile // w,)),
            dma((csize,)), dma((panels,)),
            dma((6 + tile // w,)),
        ],
        compiler_params=pltpu.CompilerParams(has_side_effects=True),
        name="exchange",
    )(hits, meta, matrix)
    metas = metas[:, 0, :]
    return pl.pallas_call(
        functools.partial(lu_kernel, dims),
        out_shape=jax.ShapeDtypeStruct(matrix.shape, f32),
        in_specs=[smem, smem] + [any_spec] * 6,
        out_specs=any_spec,
        scratch_shapes=[
            pltpu.VMEM((r_loc, c_loc, tile, tile), f32),
            pltpu.VMEM((c_loc, panels, tile, tile), f32),
            pltpu.VMEM((panels, height, tile), f32),
            pltpu.VMEM((panels, panels, tile, tile), f32),
            pltpu.VMEM((panels, tile, tile), f32),
            pltpu.VMEM((panels, tile, tile), f32),
            pltpu.VMEM((2, panels, tile, tile), bf16),
            pltpu.VMEM((2, panels, tile, tile), bf16),
            pltpu.VMEM((2, panels, panels, tile, tile), bf16),
            pltpu.VMEM((2, panels, panels, tile, tile), bf16),
            pltpu.VMEM((2, c_loc, panels * tile, tile), bf16),
            pltpu.VMEM((2, tile, panels * tile), bf16),
            pltpu.VMEM((panels, tile, tile), f32),
            pltpu.SMEM((panels,), jnp.int32),
            dma((4 + rsize,)), dma((r_loc, c_loc)),
        ],
        compiler_params=pltpu.CompilerParams(vmem_limit_bytes=60 * 1024 * 1024),
        name="factor",
    )(pivots, metas, matrix, rows, strips, cross, lower_inv, upper_inv)


def solution(mesh):
    in_specs = (P("row", "col"), P("row", None), P("row", "col", None, None), P(), P(), P())
    return jax.shard_map(
        functools.partial(body, mesh),
        mesh=mesh,
        in_specs=in_specs,
        out_specs=P("row", "col"),
        check_vma=False,
    )
```

```python
import functools

import jax
import jax.numpy as jnp
from jax import lax
from jax.experimental import pallas as pl
from jax.experimental.pallas import tpu as pltpu
from jax.sharding import PartitionSpec as P


def when(cond, fn):
    pl.when(cond)(fn)


def loop(low, high, fn):
    def one(index, carry):
        fn(index)
        return carry

    lax.fori_loop(low, high, one, 0)


def halves(value):
    high = value.astype(jnp.bfloat16)
    return high, (value - high.astype(jnp.float32)).astype(jnp.bfloat16)


def dot(left, right):
    return jnp.dot(left, right, preferred_element_type=jnp.float32)


def mm(left, right):
    (ah, al), (bh, bl) = left, right
    return dot(ah, bh) + dot(ah, bl) + dot(al, bh)


def pair(ref, *index):
    return ref[(0,) + index], ref[(1,) + index]


def lane(value, index):
    at = lax.broadcasted_iota(jnp.int32, value.shape, value.ndim - 1)
    return jnp.sum(jnp.where(at == index, value, 0.0), axis=-1, keepdims=True)


def exchange_kernel(
    dims, axes, ctl, piv, meta, mat, linv, uinv, rows, lows_out,
    matv, strips, cross, metas, sel, xcand, xgot, xfix, send1, recv1, buf2, recv2, homes, fixed_in, work,
    linvs, uinvs, lows, ups, done_low,
    m_send, m_recv, z_send, z_recv, xc_send, xc_recv, xf_send, xf_recv, ab_send, ab_recv, one_send, one_recv,
    two_send, two_recv, ag_send, ag_recv, xz_send, xz_recv, out_sem, local,
):
    panels, tile, r_loc, width, rsize, csize = dims
    c_loc = width // tile
    chips = rsize // 2
    w = width // rsize
    rr = tile // rsize
    last = panels - 1
    me = lax.axis_index("row")
    plane = lax.axis_index("col")
    chip, core = me // 2, me % 2
    lin = plane * rsize + me
    square = chips == 4
    is_holder = plane < panels

    def dev(row, col):
        return tuple(row if name == "row" else col for name in axes)

    def remote(src, dst, ssem, rsem, row, col):
        return pltpu.make_async_remote_copy(
            src_ref=src, dst_ref=dst, send_sem=ssem, recv_sem=rsem,
            device_id=dev(row, col), device_id_type=pl.DeviceIdType.MESH,
        )

    if square:
        x, y = chip % 2, chip // 2
        xn, yn = chip + 1 - 2 * x, chip + 2 - 4 * y
        to_chip = from_chip = [xn, yn, 3 - chip]
    else:
        to_chip = [(chip + d) % chips for d in range(1, chips)]
        from_chip = [(chip - d + chips) % chips for d in range(1, chips)]
    sib = chip * 2 + 1 - core

    def block(index, size):
        return pl.ds(pl.multiple_of(index * size, size), size)

    def z_own(r, up):
        return remote(
            mat.at[block(r, tile), pl.ds(0, tile)], strips.at[plane, r],
            z_send.at[1 - up, plane, r], z_recv.at[1 - up, plane, r], me, plane + 2 * up - 1,
        )

    def z_pass(n, r, up):
        return remote(
            strips.at[n, r], strips.at[n, r],
            z_send.at[1 - up, n, r], z_recv.at[1 - up, n, r], me, plane + 2 * up - 1,
        )

    def z_start(r):
        when(is_holder & (plane + 1 < csize), lambda: z_own(r, 1).start())
        when(is_holder & (plane > 0), lambda: z_own(r, 0).start())

    def z_relay(p, r):
        low, high = plane - p, plane + p

        def from_low():
            z_pass(low, r, 1).wait_recv()
            when(plane + 1 < csize, lambda: z_pass(low, r, 1).start())

        def from_high():
            z_pass(high, r, 0).wait_recv()
            when(plane > 0, lambda: z_pass(high, r, 0).start())

        when((low >= 0) & (low < panels), from_low)
        when(high < panels, from_high)

    def z_drain(p, r):
        low, high = plane - p, plane + p
        if p == 0:
            when(is_holder & (plane + 1 < csize), lambda: z_own(r, 1).wait_send())
            when(is_holder & (plane > 0), lambda: z_own(r, 0).wait_send())
        else:
            when((low >= 0) & (low < panels) & (plane + 1 < csize), lambda: z_pass(low, r, 1).wait_send())
            when((high < panels) & (plane > 0), lambda: z_pass(high, r, 0).wait_send())

    loop(0, 2, z_start)
    first_load = pltpu.make_async_copy(mat.at[:, pl.ds(0, tile)], matv.at[:, pl.ds(0, tile)], local.at[1])
    rest_load = pltpu.make_async_copy(
        mat.at[:, pl.ds(tile, width - tile)], matv.at[:, pl.ds(tile, width - tile)], local.at[2]
    )
    first_load.start()
    rest_load.start()

    def meta_copy(t):
        return remote(meta, metas.at[plane, me], m_send.at[t], m_recv.at[lin], t % rsize, t // rsize)

    def meta_in(t):
        return remote(
            meta, metas.at[t // rsize, t % rsize], m_send.at[t], m_recv.at[t], t % rsize, t // rsize
        )

    def x_give(a):
        return remote(
            xcand.at[:, block(a, rr), :], xgot.at[me], xc_send.at[a], xc_recv.at[me], a, plane
        )

    def x_got(a):
        return remote(xcand.at[:, block(a, rr), :], xgot.at[a], xc_send.at[a], xc_recv.at[a], a, plane)

    def x_fixed(slot):
        base = 0 if slot == 0 else (r_loc - 1) * tile

        def to(a):
            return remote(
                mat.at[pl.ds(pl.multiple_of(base + a * rr, rr), rr), pl.ds(0, tile)], xfix.at[slot],
                xf_send.at[slot, a], xf_recv.at[slot], a, plane,
            )

        return to

    x_top, x_bottom = x_fixed(0), x_fixed(1)
    step = 32

    def mix(values, weights):
        total = values[0] * weights[0]
        for value, weight in zip(values[1:], weights[1:]):
            total = total + value * weight
        return total

    first_load.wait()

    def x_pick(part):
        at = block(part, step)
        seen = [matv[pl.ds(pl.multiple_of(r * tile + part * step, step), step), :tile] for r in range(r_loc)]
        for s in range(2):
            xcand[s, at] = mix(seen, [ctl[s, r] for r in range(r_loc)])

    loop(0, tile // step, x_pick)

    def x_spread():
        when(me == 0, lambda: loop(1, rsize, lambda a: x_top(a).start()))
        when(me == rsize - 1, lambda: loop(0, rsize - 1, lambda a: x_bottom(a).start()))
        loop(0, rsize, lambda a: when(a != me, lambda: x_give(a).start()))

    when(is_holder, x_spread)
    loop(0, rsize * csize, lambda t: when(t != lin, lambda: meta_copy(t).start()))
    own_meta = pltpu.make_async_copy(meta, metas.at[plane, me], local.at[0])
    own_meta.start()

    def fixed(slot):
        base = 0 if slot == 0 else (r_loc - 1) * tile

        def to(a):
            return remote(
                mat.at[pl.ds(base, tile), block(a, w)], fixed_in.at[slot],
                ab_send.at[slot, a], ab_recv.at[slot], a, plane,
            )

        return to

    top, bottom = fixed(0), fixed(1)
    when(me == 0, lambda: loop(1, rsize, lambda a: top(a).start()))
    when(me == rsize - 1, lambda: loop(0, rsize - 1, lambda a: bottom(a).start()))
    high_core = (core == 0).astype(jnp.float32)
    low_core = 1.0 - high_core

    def one(s):
        return remote(send1.at[s], recv1.at[s], one_send.at[s], one_recv.at[s], sib, plane)

    def pick(part):
        at = block(part, step)
        for q in range(chips):
            even, odd = [], []
            for r in range(r_loc):
                there = pl.ds(pl.multiple_of(r * tile + part * step, step), step)
                even.append(matv[there, 2 * q * w : (2 * q + 1) * w])
                odd.append(matv[there, (2 * q + 1) * w : (2 * q + 2) * w])
            for s in range(2):
                weights = [ctl[s, r] for r in range(r_loc)]
                left, right = mix(even, weights), mix(odd, weights)
                send1[s, q, at] = left * low_core + right * high_core
                buf2[s, q, at] = left * high_core + right * low_core

    rest_load.wait()
    loop(0, tile // step, pick)
    for s in range(2):
        one(s).start()
    base = (r_loc - 1) * tile
    own_fixed = [
        pltpu.make_async_copy(matv.at[pl.ds(0, tile), pl.ds(0, w)], fixed_in.at[0], local.at[4]),
        pltpu.make_async_copy(
            matv.at[pl.ds(base, tile), pl.ds((rsize - 1) * w, w)], fixed_in.at[1], local.at[4]
        ),
    ]
    own_xfix = [
        pltpu.make_async_copy(matv.at[pl.ds(0, rr), pl.ds(0, tile)], xfix.at[0], local.at[5]),
        pltpu.make_async_copy(
            matv.at[pl.ds(base + (rsize - 1) * rr, rr), pl.ds(0, tile)], xfix.at[1], local.at[5]
        ),
    ]

    def own_z(r):
        return pltpu.make_async_copy(matv.at[block(r, tile), pl.ds(0, tile)], strips.at[plane, r], out_sem.at[r])

    for side, root in ((0, 0), (1, rsize - 1)):
        when(me == root, lambda side=side: own_fixed[side].start())
        when(is_holder & (me == root), lambda side=side: own_xfix[side].start())
    when(is_holder, lambda: loop(0, r_loc, lambda r: own_z(r).start()))

    def two(s, d):
        return remote(
            buf2.at[s, to_chip[d]], recv2.at[s, d], two_send.at[s, d], two_recv.at[s, d],
            to_chip[d] * 2 + core, plane,
        )

    def combine(s):
        one(s).wait_recv()
        for q in range(chips):
            buf2[s, q] = buf2[s, q] + recv1[s, q]

    combine(0)
    for d in range(chips - 1):
        two(0, d).start()

    def x_region(a, n):
        return cross.at[n, :, block(a, rr), :]

    def xz(d):
        return remote(
            x_region(me, plane), x_region(me, plane), xz_send.at[d], xz_recv.at[plane],
            me, (plane + d) % csize,
        )

    def x_home():
        for side, root in ((0, 0), (1, rsize - 1)):
            when(me != root, lambda side=side: (x_top if side == 0 else x_bottom)(me).wait_recv())
            when(me == root, lambda side=side: own_xfix[side].wait())
        loop(0, rsize, lambda a: when(a != me, lambda: x_got(a).wait_recv()))
        xgot[me] = xcand[:, block(me, rr), :]
        total = xgot[0]
        for a in range(1, rsize):
            total = total + xgot[a]
        slots = [xfix[0], total[0], total[1], xfix[1]]
        for k in range(panels):
            cross[plane, k, block(me, rr), :] = mix(slots, [ctl[k, r_loc + s] for s in range(panels)])
        loop(1, csize, lambda d: xz(d).start())

    when(is_holder, x_home)
    loop(2, r_loc, z_start)
    combine(1)

    def region(a, c):
        return rows.at[a, c]

    def ag(part, c, kind, a, row):
        ref = region(a, c) if part == 0 else x_region(a, c)
        return remote(ref, ref, ag_send.at[part, kind, c], ag_recv.at[part, kind, c], row, plane)

    direct = 2 if square else chips - 1
    sib_own = chips - 1
    half = panels // 2

    def peer(d):
        return from_chip[d] * 2 + core

    def ag_start(part, c):
        for d in range(direct):
            ag(part, c, d, me, to_chip[d] * 2 + core).start()
        ag(part, c, sib_own, me, sib).start()

    def ag_forward(part, c, first):
        for d in range(direct):
            ag(part, c, d, peer(d), sib).wait_recv()
            if square and first == (d == 0):
                ag(part, c, 2, peer(d), to_chip[1 - d] * 2 + core).start()
            ag(part, c, chips + d, peer(d), sib).start()

    def ag_far(part, c):
        if square:
            ag(part, c, 2, peer(2), sib).wait_recv()
            ag(part, c, chips + 2, peer(2), sib).start()

    def ag_in(part, c):
        for d in range(chips):
            kind = sib_own if d == chips - 1 else chips + d
            ag(part, c, kind, sib if d == chips - 1 else from_chip[d] * 2 + 1 - core, sib).wait_recv()

    def ag_out(part, c, first):
        ag(part, c, sib_own, me, sib).wait_send()
        for d in range(direct):
            ag(part, c, d, me, to_chip[d] * 2 + core).wait_send()
        for d in range(chips - 1):
            ag(part, c, chips + d, peer(d), sib).wait_send()
        if square:
            d = 0 if first else 1
            ag(part, c, 2, peer(d), to_chip[1 - d] * 2 + core).wait_send()

    def halved(fn):
        loop(0, half, lambda c: fn(c, True))
        loop(half, panels, lambda c: fn(c, False))

    def x_start(n):
        got = remote(x_region(me, n), x_region(me, n), xz_send.at[0], xz_recv.at[n], me, plane)
        when(plane != n, lambda: got.wait_recv())
        ag_start(1, n)

    loop(0, panels, x_start)
    for d in range(chips - 1):
        two(1, d).start()
    for r in range(2):
        z_relay(1, r)
    halved(lambda c, first: ag_forward(1, c, first))
    loop(2, r_loc, lambda r: z_relay(1, r))
    loop(0, panels, lambda c: ag_far(1, c))

    def split_inv(k):
        linvs[0, k], linvs[1, k] = halves(linv[k])
        uinvs[0, k], uinvs[1, k] = halves(uinv[k])

    loop(0, panels, split_inv)
    own_meta.wait()

    def meta_end(t):
        meta_copy(t).wait_send()
        meta_in(t).wait_recv()

    loop(0, rsize * csize, lambda t: when(t != lin, lambda: meta_end(t)))
    at_row = lax.broadcasted_iota(jnp.int32, (rsize, 8, 128), 0)
    at_sub = lax.broadcasted_iota(jnp.int32, (rsize, 8, 128), 1)
    ids = jnp.where(at_sub < r_loc, at_row * r_loc + at_sub, -1)
    for m in range(panels):
        chosen = jnp.where(ids == piv[m], 1.0, 0.0)

        def gather(n, m=m, chosen=chosen):
            found = jnp.sum(jnp.sum(chosen * metas[n], axis=0), axis=0, keepdims=True)
            sel[m, n] = found

        loop(0, csize, gather)
    loop(0, panels, lambda c: ag_in(1, c))
    halved(lambda c, first: ag_out(1, c, first))
    when(is_holder, lambda: loop(1, csize, lambda d: xz(d).wait_send()))

    def cross_panel(k):
        def low(m):
            value = mm(halves(cross[k, m]), pair(uinvs, k)) * lane(sel[m, 0], c_loc + k)
            lows[0, m, k], lows[1, m, k] = halves(value)

        def up(n):
            value = mm(pair(linvs, k), halves(cross[n, k]))
            ups[0, k, n], ups[1, k, n] = halves(value)

        loop(k + 1, panels, low)
        loop(k + 1, panels, up)

        def update(m):
            def one_tile(n):
                def go():
                    product = mm(pair(lows, m, k), pair(ups, k, n)) * lane(sel[m, n], 0)
                    cross[n, m] = cross[n, m] - product

                when(m != n, go)

            loop(k + 1, panels, one_tile)

        loop(k + 1, panels, update)

    loop(0, panels - 1, cross_panel)

    for s in range(2):
        total = buf2[s, chip]
        for d in range(chips - 1):
            two(s, d).wait_recv()
            total = total + recv2[s, d]
        homes[s] = total
    for side, root in ((0, 0), (1, rsize - 1)):
        when(me != root, lambda side=side: (top if side == 0 else bottom)(me).wait_recv())
        when(me == root, lambda side=side: own_fixed[side].wait())

    def order(part):
        at = block(part, step)
        slots = [fixed_in[0, at], homes[0, at], homes[1, at], fixed_in[1, at]]
        for k in range(panels):
            work[k, at, :w] = mix(slots, [ctl[k, r_loc + s] for s in range(panels)])

    loop(0, tile // step, order)
    column = (me * w) // tile

    def put(k):
        return pltpu.make_async_copy(work.at[k, :, pl.ds(0, w)], rows.at[me, k], local.at[6])

    def home_panel(k):
        value = mm(pair(linvs, k), halves(work[k, :, :w]))
        work[k, :, :w] = value
        put(k).start()
        opened = 1.0 - ((column == 0) & (plane <= k)).astype(jnp.float32)
        seen = halves(value)

        def update(m):
            product = mm(pair(lows, m, k), seen) * (lane(sel[m, plane], column) * opened)
            work[m, :, :w] = work[m, :, :w] - product

        loop(k + 1, panels, update)
        put(k).wait()
        ag_start(0, k)

    loop(0, panels, home_panel)

    def column_tile(r):
        def panel(k):
            value = mm(halves(work[k]), pair(uinvs, k)) * lane(meta[pl.ds(r, 1), :], c_loc + k)
            done_low[r, k] = value
            seen = halves(value * ctl[k, r_loc + panels + r])

            def update(n):
                product = mm(seen, pair(ups, k, n)) * lane(metas[n, me, pl.ds(r, 1), :], 0)
                work[n] = work[n] - product

            loop(k + 1, panels, update)

        def fetch(k):
            work[k] = strips[k, r]

        loop(0, panels, fetch)
        loop(0, panels, panel)

    def low_out(r):
        return pltpu.make_async_copy(done_low.at[r], lows_out.at[r], out_sem.at[r])

    when(is_holder, lambda: loop(0, r_loc, lambda r: own_z(r).wait()))

    def serve(r):
        for p in range(2, csize):
            z_relay(p, r)
        column_tile(r)
        low_out(r).start()

    for c in range(max(panels, r_loc)):
        if c < panels:
            ag_forward(0, c, c < half)
        if c < r_loc:
            loop(c, c + 1, serve)
    loop(0, panels, lambda c: ag_far(0, c))
    loop(0, panels, lambda c: ag_in(0, c))
    halved(lambda c, first: ag_out(0, c, first))
    for p in range(csize):
        loop(0, r_loc, lambda r, p=p: z_drain(p, r))
    for s in range(2):
        one(s).wait_send()
        for d in range(chips - 1):
            two(s, d).wait_send()
    when(me == 0, lambda: loop(1, rsize, lambda a: top(a).wait_send()))
    when(me == rsize - 1, lambda: loop(0, rsize - 1, lambda a: bottom(a).wait_send()))

    def x_spread_end():
        when(me == 0, lambda: loop(1, rsize, lambda a: x_top(a).wait_send()))
        when(me == rsize - 1, lambda: loop(0, rsize - 1, lambda a: x_bottom(a).wait_send()))
        loop(0, rsize, lambda a: when(a != me, lambda: x_give(a).wait_send()))

    when(is_holder, x_spread_end)
    loop(0, r_loc, lambda r: low_out(r).wait())


def final_kernel(dims, piv, meta, mat, rows, lows, out, matv, rowv, lowv, us, ls, row_sem, low_sem, mat_sem):
    panels, tile, r_loc, width, rsize, csize = dims
    c_loc = width // tile
    w = width // rsize
    me = lax.axis_index("row")
    plane = lax.axis_index("col")

    def tile_at(ref, i, j):
        return ref.at[pl.ds(pl.multiple_of(i * tile, tile), tile), pl.ds(pl.multiple_of(j * tile, tile), tile)]

    row_loads = []
    for a in range(rsize):
        j, off = divmod(a * w, tile)
        row_loads.append(pltpu.make_async_copy(rows.at[a], rowv.at[j, :, :, pl.ds(off, w)], row_sem.at[a]))

    def low_in(i):
        return pltpu.make_async_copy(lows.at[i], lowv.at[i], low_sem.at[i])

    def mat_in(i, j):
        return pltpu.make_async_copy(tile_at(mat, i, j), matv.at[i, j], mat_sem.at[i, j])

    def mat_out(i, j):
        return pltpu.make_async_copy(matv.at[i, j], tile_at(out, i, j), mat_sem.at[i, j])

    loop(0, 1, lambda i: low_in(i).start())
    for load in row_loads:
        load.start()
    loop(1, r_loc, lambda i: low_in(i).start())
    loop(0, r_loc, lambda i: loop(0, c_loc, lambda j: mat_in(i, j).start()))

    def gone_at(row, k):
        gone = row == piv[0]
        for m in range(1, k + 1):
            gone = gone | (row == piv[m])
        return gone

    def row_tile(i):
        low_in(i).wait()
        row = me * r_loc + i
        for k in range(panels):
            keep = jnp.where(gone_at(row, k), 0.0, 1.0).astype(jnp.float32)
            span = slice(k * tile, (k + 1) * tile)
            ls[0, :, span], ls[1, :, span] = halves(lowv[i, k] * keep)

        def target(j):
            mat_in(i, j).wait()

            def go():
                matv[i, j] = matv[i, j] - mm((ls[0], ls[1]), pair(us, j))

            when(meta[i, j] != 0, go)

        loop(0, c_loc, target)
        for k in range(panels):

            def put_low(k=k):
                matv[i, 0] = lowv[i, k]

            when((plane == k) & jnp.logical_not(gone_at(row, k)), put_low)

            def put_up(k=k):
                def one(j):
                    def go():
                        matv[i, j] = rowv[j, k]

                    when((j != 0) | (plane > k), go)

                loop(0, c_loc, one)

            when(row == piv[k], put_up)

        loop(0, c_loc, lambda j: mat_out(i, j).start())

    for load in row_loads:
        load.wait()

    def split_up(j):
        for k in range(panels):
            shown = jnp.where((j == 0) & (plane <= k), 0.0, 1.0).astype(jnp.float32)
            us[0, j, k * tile : (k + 1) * tile], us[1, j, k * tile : (k + 1) * tile] = halves(rowv[j, k] * shown)

    loop(0, c_loc, split_up)
    loop(0, r_loc, row_tile)
    loop(0, r_loc, lambda i: loop(0, c_loc, lambda j: mat_out(i, j).wait()))


def body(mesh, matrix, pattern, active, pivots, lower_inv, upper_inv):
    panels, tile = lower_inv.shape[:2]
    height, width = matrix.shape
    r_loc, c_loc = height // tile, width // tile
    rsize, csize = mesh.shape["row"], mesh.shape["col"]
    chips, w = rsize // 2, width // rsize
    rr = tile // rsize
    dims = (panels, tile, r_loc, width, rsize, csize)
    devices = rsize * csize
    f32, bf16 = jnp.float32, jnp.bfloat16

    spot = active[0, 0, :, 0] * 128 + active[0, 0, :, 1]
    places = jnp.arange(8, dtype=jnp.int32)[:, None] * 128 + jnp.arange(128, dtype=jnp.int32)[None, :]
    live = jnp.any(spot[:, None, None] == places[None], axis=0).astype(f32)
    kept = jnp.pad((pattern != 0).astype(f32), ((0, 8 - r_loc), (c_loc, 128 - c_loc - panels)))
    meta = live + kept
    ranks = jnp.sum((pivots[None, :] < pivots[:, None]).astype(jnp.int32), axis=1)
    order = ranks[:, None] == jnp.arange(panels, dtype=jnp.int32)[None, :]
    mine = lax.axis_index("row") * r_loc + jnp.arange(r_loc, dtype=jnp.int32)
    here = pivots[:, None] == mine[None, :]
    hits = jnp.any(order[:, 1:-1, None] & here[:, None, :], axis=0)
    hits = jnp.pad(hits, ((0, panels - hits.shape[0]), (0, 0)))
    upto = jnp.arange(panels)[:, None] >= jnp.arange(panels)[None, :]
    open_rows = jnp.logical_not(jnp.any(upto[:, :, None] & here[None], axis=1))
    ctl = jnp.concatenate([hits, order, open_rows], axis=1).astype(f32)

    any_spec = pl.BlockSpec(memory_space=pl.ANY)
    smem = pl.BlockSpec(memory_space=pltpu.SMEM)
    vmem = pl.BlockSpec(memory_space=pltpu.VMEM)
    dma = pltpu.SemaphoreType.DMA
    rows, lows = pl.pallas_call(
        functools.partial(exchange_kernel, dims, tuple(mesh.axis_names)),
        out_shape=[
            jax.ShapeDtypeStruct((rsize, panels, tile, w), f32),
            jax.ShapeDtypeStruct((r_loc, panels, tile, tile), f32),
        ],
        in_specs=[smem, smem, vmem, any_spec, vmem, vmem],
        out_specs=[any_spec] * 2,
        scratch_shapes=[
            pltpu.VMEM((height, width), f32),
            pltpu.VMEM((panels, r_loc, tile, tile), f32),
            pltpu.VMEM((panels, panels, tile, tile), f32),
            pltpu.VMEM((csize, rsize, 8, 128), f32),
            pltpu.VMEM((panels, csize, 1, 128), f32),
            pltpu.VMEM((2, tile, tile), f32),
            pltpu.VMEM((rsize, 2, rr, tile), f32),
            pltpu.VMEM((2, rr, tile), f32),
            pltpu.VMEM((2, chips, tile, w), f32),
            pltpu.VMEM((2, chips, tile, w), f32),
            pltpu.VMEM((2, chips, tile, w), f32),
            pltpu.VMEM((2, chips - 1, tile, w), f32),
            pltpu.VMEM((2, tile, w), f32),
            pltpu.VMEM((2, tile, w), f32),
            pltpu.VMEM((panels, tile, tile), f32),
            pltpu.VMEM((2, panels, tile, tile), bf16),
            pltpu.VMEM((2, panels, tile, tile), bf16),
            pltpu.VMEM((2, panels, panels, tile, tile), bf16),
            pltpu.VMEM((2, panels, panels, tile, tile), bf16),
            pltpu.VMEM((r_loc, panels, tile, tile), f32),
            dma((devices,)), dma((devices,)),
            dma((2, panels, r_loc)), dma((2, panels, r_loc)),
            dma((rsize,)), dma((rsize,)),
            dma((2, rsize)), dma((2,)),
            dma((2, rsize)), dma((2,)),
            dma((2,)), dma((2,)),
            dma((2, chips)), dma((2, chips)),
            dma((2, 2 * chips, panels)), dma((2, 2 * chips, panels)),
            dma((csize,)), dma((panels,)),
            dma((r_loc,)), dma((7,)),
        ],
        compiler_params=pltpu.CompilerParams(has_side_effects=True, vmem_limit_bytes=58 * 1024 * 1024),
        name="exchange",
    )(ctl, pivots, meta, matrix, lower_inv, upper_inv)
    return pl.pallas_call(
        functools.partial(final_kernel, dims),
        out_shape=jax.ShapeDtypeStruct(matrix.shape, f32),
        in_specs=[smem, smem] + [any_spec] * 3,
        out_specs=any_spec,
        scratch_shapes=[
            pltpu.VMEM((r_loc, c_loc, tile, tile), f32),
            pltpu.VMEM((c_loc, panels, tile, tile), f32),
            pltpu.VMEM((r_loc, panels, tile, tile), f32),
            pltpu.VMEM((2, c_loc, panels * tile, tile), bf16),
            pltpu.VMEM((2, tile, panels * tile), bf16),
            dma((rsize,)), dma((r_loc,)), dma((r_loc, c_loc)),
        ],
        compiler_params=pltpu.CompilerParams(vmem_limit_bytes=58 * 1024 * 1024),
        name="final",
    )(pivots, meta, matrix, rows, lows)


def solution(mesh):
    in_specs = (P("row", "col"), P("row", None), P("row", "col", None, None), P(), P(), P())
    return jax.shard_map(
        functools.partial(body, mesh),
        mesh=mesh,
        in_specs=in_specs,
        out_specs=P("row", "col"),
        check_vma=False,
    )
```

```python
import functools

import jax
import jax.numpy as jnp
from jax import lax
from jax.experimental import pallas as pl
from jax.experimental.pallas import tpu as pltpu
from jax.sharding import PartitionSpec as P


def when(cond, fn):
    pl.when(cond)(fn)


def loop(low, high, fn):
    def one(index, carry):
        fn(index)
        return carry

    lax.fori_loop(low, high, one, 0)


def halves(value):
    high = value.astype(jnp.bfloat16)
    return high, (value - high.astype(jnp.float32)).astype(jnp.bfloat16)


def dot(left, right):
    return jnp.dot(left, right, preferred_element_type=jnp.float32)


def mm(left, right):
    (ah, al), (bh, bl) = left, right
    return dot(ah, bh) + dot(ah, bl) + dot(al, bh)


def pair(ref, *index):
    return ref[(0,) + index], ref[(1,) + index]


def lane(value, index):
    at = lax.broadcasted_iota(jnp.int32, value.shape, value.ndim - 1)
    return jnp.sum(jnp.where(at == index, value, 0.0), axis=-1, keepdims=True)


def exchange_kernel(
    dims, axes, ctl, piv, meta, mat, linv, uinv, rows, lows_out,
    matv, strips, cross, metas, sel, xcand, xgot, xfix, send1, recv1, buf2, recv2, homes, fixed_in, work,
    linvs, uinvs, lows, ups, done_low,
    m_send, m_recv, z_send, z_recv, xc_send, xc_recv, xf_send, xf_recv, ab_send, ab_recv, one_send, one_recv,
    two_send, two_recv, ag_send, ag_recv, xz_send, xz_recv, out_sem, local,
):
    panels, tile, r_loc, width, rsize, csize = dims
    c_loc = width // tile
    chips = rsize // 2
    w = width // rsize
    rr = tile // rsize
    last = panels - 1
    me = lax.axis_index("row")
    plane = lax.axis_index("col")
    chip, core = me // 2, me % 2
    lin = plane * rsize + me
    square = chips == 4
    is_holder = plane < panels

    def dev(row, col):
        return tuple(row if name == "row" else col for name in axes)

    def remote(src, dst, ssem, rsem, row, col):
        return pltpu.make_async_remote_copy(
            src_ref=src, dst_ref=dst, send_sem=ssem, recv_sem=rsem,
            device_id=dev(row, col), device_id_type=pl.DeviceIdType.MESH,
        )

    if square:
        x, y = chip % 2, chip // 2
        xn, yn = chip + 1 - 2 * x, chip + 2 - 4 * y
        to_chip = from_chip = [xn, yn, 3 - chip]
    else:
        to_chip = [(chip + d) % chips for d in range(1, chips)]
        from_chip = [(chip - d + chips) % chips for d in range(1, chips)]
    sib = chip * 2 + 1 - core

    def block(index, size):
        return pl.ds(pl.multiple_of(index * size, size), size)

    def z_own(r, up):
        return remote(
            mat.at[block(r, tile), pl.ds(0, tile)], strips.at[plane, r],
            z_send.at[1 - up, plane, r], z_recv.at[1 - up, plane, r], me, plane + 2 * up - 1,
        )

    def z_pass(n, r, up):
        return remote(
            strips.at[n, r], strips.at[n, r],
            z_send.at[1 - up, n, r], z_recv.at[1 - up, n, r], me, plane + 2 * up - 1,
        )

    def z_start(r):
        when(is_holder & (plane + 1 < csize), lambda: z_own(r, 1).start())
        when(is_holder & (plane > 0), lambda: z_own(r, 0).start())

    def z_relay(p, r):
        low, high = plane - p, plane + p

        def from_low():
            z_pass(low, r, 1).wait_recv()
            when(plane + 1 < csize, lambda: z_pass(low, r, 1).start())

        def from_high():
            z_pass(high, r, 0).wait_recv()
            when(plane > 0, lambda: z_pass(high, r, 0).start())

        when((low >= 0) & (low < panels), from_low)
        when(high < panels, from_high)

    def z_drain(p, r):
        low, high = plane - p, plane + p
        if p == 0:
            when(is_holder & (plane + 1 < csize), lambda: z_own(r, 1).wait_send())
            when(is_holder & (plane > 0), lambda: z_own(r, 0).wait_send())
        else:
            when((low >= 0) & (low < panels) & (plane + 1 < csize), lambda: z_pass(low, r, 1).wait_send())
            when((high < panels) & (plane > 0), lambda: z_pass(high, r, 0).wait_send())

    loop(0, 2, z_start)
    first_load = pltpu.make_async_copy(mat.at[:, pl.ds(0, tile)], matv.at[:, pl.ds(0, tile)], local.at[1])
    rest_load = pltpu.make_async_copy(
        mat.at[:, pl.ds(tile, width - tile)], matv.at[:, pl.ds(tile, width - tile)], local.at[2]
    )
    first_load.start()
    rest_load.start()

    def meta_copy(t):
        return remote(meta, metas.at[plane, me], m_send.at[t], m_recv.at[lin], t % rsize, t // rsize)

    def meta_in(t):
        return remote(
            meta, metas.at[t // rsize, t % rsize], m_send.at[t], m_recv.at[t], t % rsize, t // rsize
        )

    def x_give(a):
        return remote(
            xcand.at[:, block(a, rr), :], xgot.at[me], xc_send.at[a], xc_recv.at[me], a, plane
        )

    def x_got(a):
        return remote(xcand.at[:, block(a, rr), :], xgot.at[a], xc_send.at[a], xc_recv.at[a], a, plane)

    def x_fixed(slot):
        base = 0 if slot == 0 else (r_loc - 1) * tile

        def to(a):
            return remote(
                mat.at[pl.ds(pl.multiple_of(base + a * rr, rr), rr), pl.ds(0, tile)], xfix.at[slot],
                xf_send.at[slot, a], xf_recv.at[slot], a, plane,
            )

        return to

    x_top, x_bottom = x_fixed(0), x_fixed(1)
    step = 32

    def mix(values, weights):
        total = values[0] * weights[0]
        for value, weight in zip(values[1:], weights[1:]):
            total = total + value * weight
        return total

    first_load.wait()

    def x_pick(part):
        at = block(part, step)
        seen = [matv[pl.ds(pl.multiple_of(r * tile + part * step, step), step), :tile] for r in range(r_loc)]
        for s in range(2):
            xcand[s, at] = mix(seen, [ctl[s, r] for r in range(r_loc)])

    loop(0, tile // step, x_pick)

    def x_spread():
        when(me == 0, lambda: loop(1, rsize, lambda a: x_top(a).start()))
        when(me == rsize - 1, lambda: loop(0, rsize - 1, lambda a: x_bottom(a).start()))
        loop(0, rsize, lambda a: when(a != me, lambda: x_give(a).start()))

    when(is_holder, x_spread)
    loop(0, rsize * csize, lambda t: when(t != lin, lambda: meta_copy(t).start()))
    own_meta = pltpu.make_async_copy(meta, metas.at[plane, me], local.at[0])
    own_meta.start()

    def fixed(slot):
        base = 0 if slot == 0 else (r_loc - 1) * tile

        def to(a):
            return remote(
                mat.at[pl.ds(base, tile), block(a, w)], fixed_in.at[slot],
                ab_send.at[slot, a], ab_recv.at[slot], a, plane,
            )

        return to

    top, bottom = fixed(0), fixed(1)
    when(me == 0, lambda: loop(1, rsize, lambda a: top(a).start()))
    when(me == rsize - 1, lambda: loop(0, rsize - 1, lambda a: bottom(a).start()))
    high_core = (core == 0).astype(jnp.float32)
    low_core = 1.0 - high_core

    def one(s):
        return remote(send1.at[s], recv1.at[s], one_send.at[s], one_recv.at[s], sib, plane)

    def pick(part):
        at = block(part, step)
        for q in range(chips):
            even, odd = [], []
            for r in range(r_loc):
                there = pl.ds(pl.multiple_of(r * tile + part * step, step), step)
                even.append(matv[there, 2 * q * w : (2 * q + 1) * w])
                odd.append(matv[there, (2 * q + 1) * w : (2 * q + 2) * w])
            for s in range(2):
                weights = [ctl[s, r] for r in range(r_loc)]
                left, right = mix(even, weights), mix(odd, weights)
                send1[s, q, at] = left * low_core + right * high_core
                buf2[s, q, at] = left * high_core + right * low_core

    rest_load.wait()
    loop(0, tile // step, pick)
    for s in range(2):
        one(s).start()
    base = (r_loc - 1) * tile
    own_fixed = [
        pltpu.make_async_copy(matv.at[pl.ds(0, tile), pl.ds(0, w)], fixed_in.at[0], local.at[4]),
        pltpu.make_async_copy(
            matv.at[pl.ds(base, tile), pl.ds((rsize - 1) * w, w)], fixed_in.at[1], local.at[4]
        ),
    ]
    own_xfix = [
        pltpu.make_async_copy(matv.at[pl.ds(0, rr), pl.ds(0, tile)], xfix.at[0], local.at[5]),
        pltpu.make_async_copy(
            matv.at[pl.ds(base + (rsize - 1) * rr, rr), pl.ds(0, tile)], xfix.at[1], local.at[5]
        ),
    ]

    def own_z(r):
        return pltpu.make_async_copy(matv.at[block(r, tile), pl.ds(0, tile)], strips.at[plane, r], out_sem.at[r])

    for side, root in ((0, 0), (1, rsize - 1)):
        when(me == root, lambda side=side: own_fixed[side].start())
        when(is_holder & (me == root), lambda side=side: own_xfix[side].start())
    when(is_holder, lambda: loop(0, r_loc, lambda r: own_z(r).start()))

    def two(s, d):
        return remote(
            buf2.at[s, to_chip[d]], recv2.at[s, d], two_send.at[s, d], two_recv.at[s, d],
            to_chip[d] * 2 + core, plane,
        )

    def combine(s):
        one(s).wait_recv()
        for q in range(chips):
            buf2[s, q] = buf2[s, q] + recv1[s, q]

    combine(0)
    for d in range(chips - 1):
        two(0, d).start()

    def spot(n, m):
        return (m - n + panels - 1) % panels

    def x_region(a, n):
        return cross.at[n, :, block(a, rr), :]

    def xz(d):
        return remote(
            x_region(me, plane), x_region(me, plane), xz_send.at[d], xz_recv.at[plane],
            me, (plane + d) % csize,
        )

    def x_home():
        for side, root in ((0, 0), (1, rsize - 1)):
            when(me != root, lambda side=side: (x_top if side == 0 else x_bottom)(me).wait_recv())
            when(me == root, lambda side=side: own_xfix[side].wait())
        loop(0, rsize, lambda a: when(a != me, lambda: x_got(a).wait_recv()))
        xgot[me] = xcand[:, block(me, rr), :]
        total = xgot[0]
        for a in range(1, rsize):
            total = total + xgot[a]
        slots = [xfix[0], total[0], total[1], xfix[1]]
        for k in range(panels):

            def keep(k=k):
                mixed = mix(slots, [ctl[k, r_loc + s] for s in range(panels)])
                cross[plane, spot(plane, k), block(me, rr), :] = mixed

            when(plane != k, keep)
        loop(1, csize, lambda d: xz(d).start())

    when(is_holder, x_home)
    loop(2, r_loc, z_start)
    combine(1)

    def region(a, c):
        return rows.at[a, c]

    def ag(part, c, kind, a, row):
        ref = region(a, c) if part == 0 else x_region(a, c)
        return remote(ref, ref, ag_send.at[part, kind, c], ag_recv.at[part, kind, c], row, plane)

    direct = 2 if square else chips - 1
    sib_own = chips - 1
    half = panels // 2

    def peer(d):
        return from_chip[d] * 2 + core

    def ag_start(part, c):
        for d in range(direct):
            ag(part, c, d, me, to_chip[d] * 2 + core).start()
        ag(part, c, sib_own, me, sib).start()

    def ag_forward(part, c, first):
        for d in range(direct):
            ag(part, c, d, peer(d), sib).wait_recv()
            if square and first == (d == 0):
                ag(part, c, 2, peer(d), to_chip[1 - d] * 2 + core).start()
            ag(part, c, chips + d, peer(d), sib).start()

    def ag_far(part, c):
        if square:
            ag(part, c, 2, peer(2), sib).wait_recv()
            ag(part, c, chips + 2, peer(2), sib).start()

    def ag_in(part, c):
        for d in range(chips):
            kind = sib_own if d == chips - 1 else chips + d
            ag(part, c, kind, sib if d == chips - 1 else from_chip[d] * 2 + 1 - core, sib).wait_recv()

    def ag_out(part, c, first):
        ag(part, c, sib_own, me, sib).wait_send()
        for d in range(direct):
            ag(part, c, d, me, to_chip[d] * 2 + core).wait_send()
        for d in range(chips - 1):
            ag(part, c, chips + d, peer(d), sib).wait_send()
        if square:
            d = 0 if first else 1
            ag(part, c, 2, peer(d), to_chip[1 - d] * 2 + core).wait_send()

    def halved(fn):
        loop(0, half, lambda c: fn(c, True))
        loop(half, panels, lambda c: fn(c, False))

    def x_start(n):
        got = remote(x_region(me, n), x_region(me, n), xz_send.at[0], xz_recv.at[n], me, plane)
        when(plane != n, lambda: got.wait_recv())
        ag_start(1, n)

    loop(0, panels, x_start)
    for r in range(2):
        z_relay(1, r)
    halved(lambda c, first: ag_forward(1, c, first))
    for d in range(chips - 1):
        two(1, d).start()
    loop(2, r_loc, lambda r: z_relay(1, r))
    loop(0, panels, lambda c: ag_far(1, c))

    def split_inv(k):
        linvs[0, k], linvs[1, k] = halves(linv[k])
        uinvs[0, k], uinvs[1, k] = halves(uinv[k])

    loop(0, panels, split_inv)
    own_meta.wait()

    def meta_end(t):
        meta_copy(t).wait_send()
        meta_in(t).wait_recv()

    loop(0, rsize * csize, lambda t: when(t != lin, lambda: meta_end(t)))
    at_row = lax.broadcasted_iota(jnp.int32, (rsize, 8, 128), 0)
    at_sub = lax.broadcasted_iota(jnp.int32, (rsize, 8, 128), 1)
    ids = jnp.where(at_sub < r_loc, at_row * r_loc + at_sub, -1)
    for m in range(panels):
        chosen = jnp.where(ids == piv[m], 1.0, 0.0)

        def gather(n, m=m, chosen=chosen):
            found = jnp.sum(jnp.sum(chosen * metas[n], axis=0), axis=0, keepdims=True)
            sel[m, n] = found

        loop(0, csize, gather)
    loop(0, panels, lambda c: ag_in(1, c))
    halved(lambda c, first: ag_out(1, c, first))
    when(is_holder, lambda: loop(1, csize, lambda d: xz(d).wait_send()))

    def cross_panel(k):
        def low(m):
            value = mm(halves(cross[k, spot(k, m)]), pair(uinvs, k)) * lane(sel[m, 0], c_loc + k)
            lows[0, m, k], lows[1, m, k] = halves(value)

        def up(n):
            value = mm(pair(linvs, k), halves(cross[n, spot(n, k)]))
            ups[0, k, n], ups[1, k, n] = halves(value)

        loop(k + 1, panels, low)
        loop(k + 1, panels, up)

        def update(m):
            def one_tile(n):
                def go():
                    product = mm(pair(lows, m, k), pair(ups, k, n)) * lane(sel[m, n], 0)
                    cross[n, spot(n, m)] = cross[n, spot(n, m)] - product

                when(m != n, go)

            loop(k + 1, panels, one_tile)

        loop(k + 1, panels, update)

    loop(0, panels - 1, cross_panel)
    loop(0, 2, lambda r: z_relay(2, r))

    for s in range(2):
        total = buf2[s, chip]
        for d in range(chips - 1):
            two(s, d).wait_recv()
            total = total + recv2[s, d]
        homes[s] = total
    for side, root in ((0, 0), (1, rsize - 1)):
        when(me != root, lambda side=side: (top if side == 0 else bottom)(me).wait_recv())
        when(me == root, lambda side=side: own_fixed[side].wait())

    def order(part):
        at = block(part, step)
        slots = [fixed_in[0, at], homes[0, at], homes[1, at], fixed_in[1, at]]
        for k in range(panels):
            work[k, at, :w] = mix(slots, [ctl[k, r_loc + s] for s in range(panels)])

    loop(0, tile // step, order)
    column = (me * w) // tile

    def put(k):
        return pltpu.make_async_copy(work.at[k, :, pl.ds(0, w)], rows.at[me, k], local.at[6])

    def home_panel(k):
        value = mm(pair(linvs, k), halves(work[k, :, :w]))
        work[k, :, :w] = value
        put(k).start()
        opened = 1.0 - ((column == 0) & (plane <= k)).astype(jnp.float32)
        seen = halves(value)

        def update(m):
            product = mm(pair(lows, m, k), seen) * (lane(sel[m, plane], column) * opened)
            work[m, :, :w] = work[m, :, :w] - product

        loop(k + 1, panels, update)
        put(k).wait()
        ag_start(0, k)

    loop(0, panels, home_panel)
    loop(2, r_loc, lambda r: z_relay(2, r))

    def column_tile(r):
        def panel(k):
            value = mm(halves(work[k]), pair(uinvs, k)) * lane(meta[pl.ds(r, 1), :], c_loc + k)
            done_low[r, k] = value
            seen = halves(value * ctl[k, r_loc + panels + r])

            def update(n):
                product = mm(seen, pair(ups, k, n)) * lane(metas[n, me, pl.ds(r, 1), :], 0)
                work[n] = work[n] - product

            loop(k + 1, panels, update)

        def fetch(k):
            work[k] = strips[k, r]

        loop(0, panels, fetch)
        loop(0, panels, panel)

    def low_out(r):
        return pltpu.make_async_copy(done_low.at[r], lows_out.at[r], out_sem.at[r])

    when(is_holder, lambda: loop(0, r_loc, lambda r: own_z(r).wait()))

    def serve(r):
        for p in range(3, csize):
            z_relay(p, r)
        column_tile(r)
        low_out(r).start()

    for c in range(max(panels, r_loc)):
        if c < panels:
            ag_forward(0, c, c < half)
        if c < r_loc:
            loop(c, c + 1, serve)
    loop(0, panels, lambda c: ag_far(0, c))
    loop(0, panels, lambda c: ag_in(0, c))
    halved(lambda c, first: ag_out(0, c, first))
    for p in range(csize):
        loop(0, r_loc, lambda r, p=p: z_drain(p, r))
    for s in range(2):
        one(s).wait_send()
        for d in range(chips - 1):
            two(s, d).wait_send()
    when(me == 0, lambda: loop(1, rsize, lambda a: top(a).wait_send()))
    when(me == rsize - 1, lambda: loop(0, rsize - 1, lambda a: bottom(a).wait_send()))

    def x_spread_end():
        when(me == 0, lambda: loop(1, rsize, lambda a: x_top(a).wait_send()))
        when(me == rsize - 1, lambda: loop(0, rsize - 1, lambda a: x_bottom(a).wait_send()))
        loop(0, rsize, lambda a: when(a != me, lambda: x_give(a).wait_send()))

    when(is_holder, x_spread_end)
    loop(0, r_loc, lambda r: low_out(r).wait())


def final_kernel(dims, piv, meta, mat, rows, lows, out, matv, rowv, lowv, us, ls, row_sem, low_sem, mat_sem):
    panels, tile, r_loc, width, rsize, csize = dims
    c_loc = width // tile
    w = width // rsize
    me = lax.axis_index("row")
    plane = lax.axis_index("col")

    def tile_at(ref, i, j):
        return ref.at[pl.ds(pl.multiple_of(i * tile, tile), tile), pl.ds(pl.multiple_of(j * tile, tile), tile)]

    row_loads = []
    for a in range(rsize):
        j, off = divmod(a * w, tile)
        row_loads.append(pltpu.make_async_copy(rows.at[a], rowv.at[j, :, :, pl.ds(off, w)], row_sem.at[a]))

    def low_in(i):
        return pltpu.make_async_copy(lows.at[i], lowv.at[i], low_sem.at[i])

    def mat_in(i, j):
        return pltpu.make_async_copy(tile_at(mat, i, j), matv.at[i, j], mat_sem.at[i, j])

    def mat_out(i, j):
        return pltpu.make_async_copy(matv.at[i, j], tile_at(out, i, j), mat_sem.at[i, j])

    loop(0, 1, lambda i: low_in(i).start())
    for load in row_loads:
        load.start()
    loop(1, r_loc, lambda i: low_in(i).start())
    loop(0, r_loc, lambda i: loop(0, c_loc, lambda j: mat_in(i, j).start()))

    def gone_at(row, k):
        gone = row == piv[0]
        for m in range(1, k + 1):
            gone = gone | (row == piv[m])
        return gone

    def row_tile(i):
        low_in(i).wait()
        row = me * r_loc + i
        for k in range(panels):
            keep = jnp.where(gone_at(row, k), 0.0, 1.0).astype(jnp.float32)
            span = slice(k * tile, (k + 1) * tile)
            ls[0, :, span], ls[1, :, span] = halves(lowv[i, k] * keep)

        def target(j):
            mat_in(i, j).wait()

            def go():
                matv[i, j] = matv[i, j] - mm((ls[0], ls[1]), pair(us, j))

            when(meta[i, j] != 0, go)

        loop(0, c_loc, target)
        for k in range(panels):

            def put_low(k=k):
                matv[i, 0] = lowv[i, k]

            when((plane == k) & jnp.logical_not(gone_at(row, k)), put_low)

            def put_up(k=k):
                def one(j):
                    def go():
                        matv[i, j] = rowv[j, k]

                    when((j != 0) | (plane > k), go)

                loop(0, c_loc, one)

            when(row == piv[k], put_up)

        loop(0, c_loc, lambda j: mat_out(i, j).start())

    for load in row_loads:
        load.wait()

    def split_up(j):
        for k in range(panels):
            shown = jnp.where((j == 0) & (plane <= k), 0.0, 1.0).astype(jnp.float32)
            us[0, j, k * tile : (k + 1) * tile], us[1, j, k * tile : (k + 1) * tile] = halves(rowv[j, k] * shown)

    loop(0, c_loc, split_up)
    loop(0, r_loc, row_tile)
    loop(0, r_loc, lambda i: loop(0, c_loc, lambda j: mat_out(i, j).wait()))


def body(mesh, matrix, pattern, active, pivots, lower_inv, upper_inv):
    panels, tile = lower_inv.shape[:2]
    height, width = matrix.shape
    r_loc, c_loc = height // tile, width // tile
    rsize, csize = mesh.shape["row"], mesh.shape["col"]
    chips, w = rsize // 2, width // rsize
    rr = tile // rsize
    dims = (panels, tile, r_loc, width, rsize, csize)
    devices = rsize * csize
    f32, bf16 = jnp.float32, jnp.bfloat16

    spot = active[0, 0, :, 0] * 128 + active[0, 0, :, 1]
    places = jnp.arange(8, dtype=jnp.int32)[:, None] * 128 + jnp.arange(128, dtype=jnp.int32)[None, :]
    live = jnp.any(spot[:, None, None] == places[None], axis=0).astype(f32)
    kept = jnp.pad((pattern != 0).astype(f32), ((0, 8 - r_loc), (c_loc, 128 - c_loc - panels)))
    meta = live + kept
    ranks = jnp.sum((pivots[None, :] < pivots[:, None]).astype(jnp.int32), axis=1)
    order = ranks[:, None] == jnp.arange(panels, dtype=jnp.int32)[None, :]
    mine = lax.axis_index("row") * r_loc + jnp.arange(r_loc, dtype=jnp.int32)
    here = pivots[:, None] == mine[None, :]
    hits = jnp.any(order[:, 1:-1, None] & here[:, None, :], axis=0)
    hits = jnp.pad(hits, ((0, panels - hits.shape[0]), (0, 0)))
    upto = jnp.arange(panels)[:, None] >= jnp.arange(panels)[None, :]
    open_rows = jnp.logical_not(jnp.any(upto[:, :, None] & here[None], axis=1))
    ctl = jnp.concatenate([hits, order, open_rows], axis=1).astype(f32)

    any_spec = pl.BlockSpec(memory_space=pl.ANY)
    smem = pl.BlockSpec(memory_space=pltpu.SMEM)
    vmem = pl.BlockSpec(memory_space=pltpu.VMEM)
    dma = pltpu.SemaphoreType.DMA
    rows, lows = pl.pallas_call(
        functools.partial(exchange_kernel, dims, tuple(mesh.axis_names)),
        out_shape=[
            jax.ShapeDtypeStruct((rsize, panels, tile, w), f32),
            jax.ShapeDtypeStruct((r_loc, panels, tile, tile), f32),
        ],
        in_specs=[smem, smem, vmem, any_spec, vmem, vmem],
        out_specs=[any_spec] * 2,
        scratch_shapes=[
            pltpu.VMEM((height, width), f32),
            pltpu.VMEM((panels, r_loc, tile, tile), f32),
            pltpu.VMEM((panels, panels - 1, tile, tile), f32),
            pltpu.VMEM((csize, rsize, 8, 128), f32),
            pltpu.VMEM((panels, csize, 1, 128), f32),
            pltpu.VMEM((2, tile, tile), f32),
            pltpu.VMEM((rsize, 2, rr, tile), f32),
            pltpu.VMEM((2, rr, tile), f32),
            pltpu.VMEM((2, chips, tile, w), f32),
            pltpu.VMEM((2, chips, tile, w), f32),
            pltpu.VMEM((2, chips, tile, w), f32),
            pltpu.VMEM((2, chips - 1, tile, w), f32),
            pltpu.VMEM((2, tile, w), f32),
            pltpu.VMEM((2, tile, w), f32),
            pltpu.VMEM((panels, tile, tile), f32),
            pltpu.VMEM((2, panels, tile, tile), bf16),
            pltpu.VMEM((2, panels, tile, tile), bf16),
            pltpu.VMEM((2, panels, panels, tile, tile), bf16),
            pltpu.VMEM((2, panels, panels, tile, tile), bf16),
            pltpu.VMEM((r_loc, panels, tile, tile), f32),
            dma((devices,)), dma((devices,)),
            dma((2, panels, r_loc)), dma((2, panels, r_loc)),
            dma((rsize,)), dma((rsize,)),
            dma((2, rsize)), dma((2,)),
            dma((2, rsize)), dma((2,)),
            dma((2,)), dma((2,)),
            dma((2, chips)), dma((2, chips)),
            dma((2, 2 * chips, panels)), dma((2, 2 * chips, panels)),
            dma((csize,)), dma((panels,)),
            dma((r_loc,)), dma((7,)),
        ],
        compiler_params=pltpu.CompilerParams(has_side_effects=True, vmem_limit_bytes=58 * 1024 * 1024),
        name="exchange",
    )(ctl, pivots, meta, matrix, lower_inv, upper_inv)
    return pl.pallas_call(
        functools.partial(final_kernel, dims),
        out_shape=jax.ShapeDtypeStruct(matrix.shape, f32),
        in_specs=[smem, smem] + [any_spec] * 3,
        out_specs=any_spec,
        scratch_shapes=[
            pltpu.VMEM((r_loc, c_loc, tile, tile), f32),
            pltpu.VMEM((c_loc, panels, tile, tile), f32),
            pltpu.VMEM((r_loc, panels, tile, tile), f32),
            pltpu.VMEM((2, c_loc, panels * tile, tile), bf16),
            pltpu.VMEM((2, tile, panels * tile), bf16),
            dma((rsize,)), dma((r_loc,)), dma((r_loc, c_loc)),
        ],
        compiler_params=pltpu.CompilerParams(vmem_limit_bytes=58 * 1024 * 1024),
        name="final",
    )(pivots, meta, matrix, rows, lows)


def solution(mesh):
    in_specs = (P("row", "col"), P("row", None), P("row", "col", None, None), P(), P(), P())
    return jax.shard_map(
        functools.partial(body, mesh),
        mesh=mesh,
        in_specs=in_specs,
        out_specs=P("row", "col"),
        check_vma=False,
    )
```
